128 devices in a mesh: gx: 8 (over z_lo, x), gy: 4 (over z_hi, core), gz: 4 (over y).
Axes of the slice: x: 4, y: 4, z: 4 (z_hi: 2, z_lo: 2; z = z_hi * 2 + z_lo), core: 2. Of those that a mesh axis runs over, the one named last changes fastest.
Arguments:
- x_saved: bfloat16 [1024, 16384], P('gx', ('gy', 'gz')), may hold values from -0.1875 to 0.1875
- grad_out: bfloat16 [1024, 28672], P('gx', ('gz', 'gy')), may hold values from -6 to 6
- weight: bfloat16 [16384, 28672], P('gy', ('gz', 'gx')), may hold values from -0.09375 to 0.09375
Outputs:
- grad_in: bfloat16 [1024, 16384], P('gx', ('gy', 'gz'))
- grad_weight: bfloat16 [16384, 28672], P('gy', ('gz', 'gx'))
The draws below stay inside these ranges and needn't reach their ends.
All inputs are finite; a program needn't handle non-finite values.
Results may differ from the reference program's by a relative error of at most 0.001.
Values may be sent and summed in bfloat16 or wider, within the bound.
A program may use at most 128 MiB of HBM per device.

```python
import jax
import jax.numpy as jnp

D = 16384
FFW = 28672
TOKENS = 1024


def spiked(entries, rng, source, target, parts, factor):
    def block_of(dim):
        return (jnp.arange(entries.shape[dim]) // (entries.shape[dim] // parts)).reshape((-1,) + (1,) * (entries.ndim - 1 - dim))

    near = jax.random.permutation(rng, parts)[block_of(target)]
    second = (block_of(target) + parts // 2) % parts
    return jnp.where((block_of(source) == near) | (block_of(source) == second), factor * entries, entries)


def shard_levels(rng, dims, cuts, smallest, top_value):
    factor_of = 1.0
    for dim, parts in cuts:
        draws = jax.random.uniform(jax.random.fold_in(jax.random.fold_in(rng, 6), dim), (parts,), jnp.float32, smallest / len(cuts), top_value / len(cuts))
        factor_of = factor_of * jnp.repeat(jnp.exp(draws), dims[dim] // parts).reshape((-1,) + (1,) * (len(dims) - 1 - dim))
    return factor_of


def noise(own_key, shape, deviation, reach, shards=(), held_as=jnp.bfloat16):
    values = jax.random.normal(own_key, shape, jnp.float32) * deviation
    if len(shards) > 0:
        values = shard_levels(own_key, shape, shards, -0.22, 0.18) * values
    return jnp.clip(values, min=-reach, max=reach).astype(held_as)


def gaussian_with(key, extent, width, limit, pieces, heavy, kind=jnp.bfloat16):
    result = width * jax.random.normal(key, extent, jnp.float32)
    if pieces:
        result = result * shard_levels(key, extent, pieces, -0.22, 0.18)
    return jnp.clip(spiked(result, jax.random.fold_in(key, 3), *heavy), -limit, limit).astype(kind)


def setup_inputs(seed: int = 0) -> dict:
    arg_keys = jax.random.split(jax.random.key(seed), 4)
    x_saved = noise(arg_keys[0], (TOKENS, D), (1.0 / (TOKENS ** 0.5)), 0.1875, ((0, 8), (1, 16)))
    grad_out = noise(arg_keys[1], (TOKENS, FFW), 1.0, 6.0, ((0, 8), (1, 16)))
    weight = gaussian_with(arg_keys[2], (D, FFW), D ** -0.5, 0.09375, ((0, 4), (1, 32)), (1, 0, 32, 2.75))
    return dict(x_saved=x_saved, grad_out=grad_out, weight=weight)


def reference(x_saved, grad_out, weight):
    grad_in = jnp.dot(grad_out, weight.T, preferred_element_type=jnp.float32).astype(jnp.bfloat16)
    grad_weight = jnp.dot(x_saved.T, grad_out, preferred_element_type=jnp.float32).astype(jnp.bfloat16)
    return grad_in, grad_weight
```

```python
import functools

import jax
import jax.numpy as jnp
from jax import lax
from jax.experimental import pallas as pl
from jax.experimental.pallas import tpu as pltpu
from jax.sharding import PartitionSpec as P

SIZE = {"x": 4, "y": 4, "z": 2}
AXES = ("x", "y", "z")
ROWS = ((0, 256), (256, 384), (640, 384))
GATHER_ORDER = (("x", "y", "z"), ("y", "z", "x"), ("z", "x", "y"))
REDUCE_ORDER = (("y", "x", "z"), ("x", "z", "y"), ("z", "y", "x"))
OFFSETS = tuple((a, b, c) for a in range(4) for b in range(4) for c in range(2))


def index_of(off):
    return (off[0] * 4 + off[1]) * 2 + off[2]


def children(order, off):
    at = dict(zip(AXES, off))
    last = max([i for i in range(3) if at[order[i]]], default=-1)
    found = []

    def child(axis, value):
        moved = dict(at)
        moved[axis] = value
        return tuple(moved[a] for a in AXES)

    if last >= 0 and SIZE[order[last]] == 4:
        axis = order[last]
        if at[axis] == 1:
            found.append((child(axis, 2), axis, 1, 0))
        if at[axis] == 3:
            found.append((child(axis, 2), axis, -1, 1))
    for i in range(last + 1, 3):
        axis = order[i]
        found.append((child(axis, 1), axis, 1, None))
        if SIZE[axis] == 4:
            found.append((child(axis, 3), axis, -1, None))
    return found


def parents(order):
    found = {}
    for off in OFFSETS:
        for kid, axis, step, half in children(order, off):
            found.setdefault(kid, []).append((off, axis, step, half))
    return found


def span(color, half):
    start, rows = ROWS[color]
    if half is None:
        return start, rows
    return start + half * (rows // 2), rows // 2


def plan(wire_bytes, rate=46500.0, delay=1.8, g_time=12.0):
    free = {("x", 1): g_time * 0.8, ("x", -1): g_time * 0.8, ("y", 1): 2.0, ("y", -1): 2.0, ("z", 1): g_time * 0.8}
    arrive = {}

    def send(kind, color, kid, axis, step, half, now, nbytes):
        link = (axis, step if SIZE[axis] == 4 else 1)
        free[link] = max(free[link], now) + nbytes / rate
        arrive[(kind, color, kid, half)] = free[link] + delay

    tasks = {}
    up = [parents(order) for order in REDUCE_ORDER]
    gather_up = [parents(order) for order in GATHER_ORDER]
    for color in range(3):
        for off in OFFSETS:
            tasks[("ag", color, off)] = None
            tasks[("rs", color, off)] = None
    for oy in range(4):
        for color in range(3):
            tasks[("gw", color, oy)] = None
    for ox in range(4):
        for oy in range(4):
            tasks[("pp", ox, oy)] = None
    distance = (0, 1, 2, 1)
    done = {}
    now = 2.0
    program = []

    def ready(task):
        kind, first, off = task
        if kind == "ag":
            if off == (0, 0, 0):
                return 2.0
            need = [("ag", first, off, half) for _, _, _, half in gather_up[first][off]]
            if any(n not in arrive for n in need):
                return None
            return max(arrive[n] for n in need)
        if kind == "rs":
            if ("pp", off[0], off[1]) not in done:
                return None
            need = [("rs", first, kid, half) for kid, _, _, half in children(REDUCE_ORDER[first], off)]
            if any(n not in arrive for n in need):
                return None
            return max([arrive[n] for n in need], default=0.0)
        if kind == "pp":
            return g_time
        if any(("ag", first, (a, off, c)) not in done for a in range(4) for c in range(2)):
            return None
        return g_time

    def rank(task, at):
        kind = task[0]
        if kind in ("ag", "rs"):
            return (0, at, str(task))
        if kind == "pp":
            return (1, -(distance[task[1]] + distance[task[2]]), str(task))
        return (2, 0.0, str(task))

    while tasks:
        options = [(ready(t), t) for t in tasks]
        options = [(r, t) for r, t in options if r is not None]
        open_now = [(r, t) for r, t in options if r <= now]
        if not open_now:
            now = min(r for r, _ in options)
            continue
        _, task = min(open_now, key=lambda item: rank(item[1], item[0]))
        del tasks[task]
        program.append(task)
        kind, first, off = task
        now += {"ag": 0.05, "rs": 0.1, "pp": 0.85, "gw": 1.3}[kind]
        done[task] = now
        if kind == "ag":
            for kid, axis, step, half in children(GATHER_ORDER[first], off):
                send("ag", first, kid, axis, step, half, now, span(first, half)[1] * 256)
        if kind == "rs" and off != (0, 0, 0):
            for _, axis, step, half in up[first][off]:
                send("rs", first, off, axis, -step, half, now, span(first, half)[1] * 128 * wire_bytes)
    return program, now


def body(x_ref, go_ref, w_ref, gi_ref, gw_ref, w_buf, x_all, g_all, part, landed, stage,
         w_sem, ag_send, ag_recv, rs_send, rs_recv, g_send, g_recv, h_send, out_sem, *, program):
    gx, gy, y = lax.axis_index("gx"), lax.axis_index("gy"), lax.axis_index("gz")
    zl, x = gx // 4, gx % 4
    zh, core = gy // 2, gy % 2

    def neighbour(axis, step):
        if axis == "x":
            return {"gx": zl * 4 + (x + step + 4) % 4, "gy": gy, "gz": y}
        if axis == "y":
            return {"gx": gx, "gy": gy, "gz": (y + step + 4) % 4}
        return {"gx": (1 - zl) * 4 + x, "gy": gy, "gz": y}

    def remote(src, dst, send_sem, recv_sem, device):
        return pltpu.make_async_remote_copy(
            src_ref=src, dst_ref=dst, send_sem=send_sem, recv_sem=recv_sem,
            device_id=device, device_id_type=pl.DeviceIdType.MESH)

    w_copy = pltpu.make_async_copy(w_ref, w_buf, w_sem)
    w_copy.start()

    for half in range(2):
        for far in range(2):
            to_x, to_y = zh * 4 + 2 * core + half, far * 2 + zl
            src = go_ref.at[:, pl.ds(half * 896, 896)]
            here = jnp.logical_and(to_x == gx, to_y == gy)

            @pl.when(here)
            def _():
                pltpu.make_async_copy(src, g_all.at[gx], g_recv.at[gx]).start()

            @pl.when(jnp.logical_not(here))
            def _():
                remote(src, g_all.at[gx], g_send.at[2 * half + far], g_recv.at[gx],
                       {"gx": to_x, "gy": to_y, "gz": y}).start()

    own = gx * 4 + y
    x_all[own] = x_ref[...].T

    def gather_slot(off):
        return ((zl + off[2]) % 2 * 4 + (x + 4 - off[0]) % 4) * 4 + (y + 4 - off[1]) % 4

    gather_up = [parents(order) for order in GATHER_ORDER]
    reduce_up = [parents(order) for order in REDUCE_ORDER]

    def sem_id(color, off, half):
        return (color * 32 + index_of(off)) * 2 + (half or 0)

    def gather(color, off):
        slot = gather_slot(off)
        if off != (0, 0, 0):
            for _, axis, step, half in gather_up[color][off]:
                start, rows = span(color, half)
                view = x_all.at[slot, pl.ds(start, rows), :]
                remote(view, view, ag_send, ag_recv.at[sem_id(color, off, half)], neighbour(axis, -step)).wait_recv()
        for kid, axis, step, half in children(GATHER_ORDER[color], off):
            start, rows = span(color, half)
            view = x_all.at[slot, pl.ds(start, rows), :]
            remote(view, view, ag_send, ag_recv.at[sem_id(color, kid, half)], neighbour(axis, step)).start()

    def products(ox, oy):
        to_x, to_y = (x + 4 - ox) % 4, (y + 4 - oy) % 4
        units = jnp.concatenate([g_all[zl * 4 + to_x], g_all[(1 - zl) * 4 + to_x]], axis=0)
        base = index_of((ox, oy, 0))

        def tile(i, carry):
            lines = pl.ds(pl.multiple_of(to_y * 1024 + i * 256, 256), 256)
            got = lax.dot_general(w_buf[lines, :], units, (((1,), (1,)), ((), ())),
                                  preferred_element_type=jnp.float32)
            into = pl.ds(pl.multiple_of(i * 256, 256), 256)
            part[base, into, :] = got[:, :128]
            part[base + 1, into, :] = got[:, 128:]
            return carry

        lax.fori_loop(0, 4, tile, 0)

    def reduce(color, off):
        at = index_of(off)
        for kid, axis, step, half in children(REDUCE_ORDER[color], off):
            start, rows = span(color, half)
            src = landed.at[index_of(kid), pl.ds(start, rows), :]
            remote(src, src, rs_send, rs_recv.at[sem_id(color, kid, half)], neighbour(axis, step)).wait_recv()
            part[at, pl.ds(start, rows), :] = part[at, pl.ds(start, rows), :] + landed[index_of(kid), pl.ds(start, rows), :]
        if off != (0, 0, 0):
            for _, axis, step, half in reduce_up[color][off]:
                start, rows = span(color, half)
                remote(part.at[at, pl.ds(start, rows), :], landed.at[at, pl.ds(start, rows), :], rs_send,
                       rs_recv.at[sem_id(color, off, half)], neighbour(axis, -step)).start()

    staged = []

    def weights(color, oy):
        start, rows = ROWS[color]
        from_y = (y + 4 - oy) % 4
        slot = len(staged) % 2
        if len(staged) >= 2:
            staged[-2].wait()
        left = jnp.concatenate([x_all[i * 4 + from_y, pl.ds(start, rows), :] for i in range(8)], axis=1)
        got = jnp.dot(left, g_all[...].reshape(1024, 896), preferred_element_type=jnp.float32)
        stage[slot, pl.ds(0, rows), :] = got.astype(jnp.bfloat16)
        copy = pltpu.make_async_copy(
            stage.at[slot, pl.ds(0, rows), :],
            gw_ref.at[pl.ds(pl.multiple_of(from_y * 1024 + start, 128), rows), :], out_sem.at[slot])
        copy.start()
        staged.append(copy)

    fetched = False

    def fetch():
        for i in range(4):
            slot = core * 4 + i
            pltpu.make_async_copy(g_all.at[slot], g_all.at[slot], g_recv.at[slot]).wait()
            remote(g_all.at[slot], g_all.at[slot], h_send.at[i], g_recv.at[slot],
                   {"gx": gx, "gy": zh * 2 + 1 - core, "gz": y}).start()
        for i in range(4):
            slot = (1 - core) * 4 + i
            pltpu.make_async_copy(g_all.at[slot], g_all.at[slot], g_recv.at[slot]).wait()
        w_copy.wait()

    for kind, first, off in program:
        if kind == "ag":
            gather(first, off)
        elif kind == "rs":
            reduce(first, off)
        else:
            if not fetched:
                fetch()
                fetched = True
            if kind == "pp":
                products(first, off)
            else:
                weights(first, off)

    gi_ref[...] = part[0].T.astype(jnp.bfloat16)

    for copy in staged[-2:]:
        copy.wait()
    for half in range(2):
        for far in range(2):
            to_x, to_y = zh * 4 + 2 * core + half, far * 2 + zl
            src = go_ref.at[:, pl.ds(half * 896, 896)]

            @pl.when(jnp.logical_not(jnp.logical_and(to_x == gx, to_y == gy)))
            def _():
                remote(src, g_all.at[gx], g_send.at[2 * half + far], g_recv.at[gx],
                       {"gx": to_x, "gy": to_y, "gz": y}).wait_send()
    for i in range(4):
        slot = core * 4 + i
        remote(g_all.at[slot], g_all.at[slot], h_send.at[i], g_recv.at[slot],
               {"gx": gx, "gy": zh * 2 + 1 - core, "gz": y}).wait_send()
    sent = x_all.at[pl.ds(0, 31)]
    pltpu.make_async_copy(sent, sent, ag_send).wait()
    sent = part.at[pl.ds(0, 31)]
    pltpu.make_async_copy(sent, sent, rs_send).wait()


def local(x_saved, grad_out, weight):
    program, _ = plan(4)
    vmem = pl.BlockSpec(memory_space=pltpu.VMEM)
    anywhere = pl.BlockSpec(memory_space=pl.ANY)
    return pl.pallas_call(
        functools.partial(body, program=program),
        out_shape=(jax.ShapeDtypeStruct((128, 1024), jnp.bfloat16),
                   jax.ShapeDtypeStruct((4096, 896), jnp.bfloat16)),
        in_specs=[vmem, vmem, anywhere],
        out_specs=(vmem, anywhere),
        scratch_shapes=[
            pltpu.VMEM((4096, 896), jnp.bfloat16),
            pltpu.VMEM((32, 1024, 128), jnp.bfloat16),
            pltpu.VMEM((8, 128, 896), jnp.bfloat16),
            pltpu.VMEM((32, 1024, 128), jnp.float32),
            pltpu.VMEM((32, 1024, 128), jnp.float32),
            pltpu.VMEM((2, 384, 896), jnp.bfloat16),
            pltpu.SemaphoreType.DMA,
            pltpu.SemaphoreType.DMA,
            pltpu.SemaphoreType.DMA((192,)),
            pltpu.SemaphoreType.DMA,
            pltpu.SemaphoreType.DMA((192,)),
            pltpu.SemaphoreType.DMA((4,)),
            pltpu.SemaphoreType.DMA((8,)),
            pltpu.SemaphoreType.DMA((4,)),
            pltpu.SemaphoreType.DMA((2,)),
        ],
        compiler_params=pltpu.CompilerParams(has_side_effects=True, vmem_limit_bytes=67043328),
    )(x_saved, grad_out, weight)


def solution(mesh):
    return jax.shard_map(
        local,
        mesh=mesh,
        in_specs=(P("gx", ("gy", "gz")), P("gx", ("gz", "gy")), P("gy", ("gz", "gx"))),
        out_specs=(P("gx", ("gy", "gz")), P("gy", ("gz", "gx"))),
        check_vma=False,
    )
```

```python
import functools

import jax
import jax.numpy as jnp
from jax import lax
from jax.experimental import pallas as pl
from jax.experimental.pallas import tpu as pltpu
from jax.sharding import PartitionSpec as P

SIZE = {"x": 4, "y": 4, "z": 2}
AXES = ("x", "y", "z")
ROWS = ((0, 256), (256, 384), (640, 384))
GATHER_ORDER = (("x", "y", "z"), ("y", "z", "x"), ("z", "x", "y"))
REDUCE_ORDER = (("y", "x", "z"), ("x", "z", "y"), ("z", "y", "x"))
OFFSETS = tuple((a, b, c) for a in range(4) for b in range(4) for c in range(2))


def index_of(off):
    return (off[0] * 4 + off[1]) * 2 + off[2]


def children(order, off):
    at = dict(zip(AXES, off))
    last = max([i for i in range(3) if at[order[i]]], default=-1)
    found = []

    def child(axis, value):
        moved = dict(at)
        moved[axis] = value
        return tuple(moved[a] for a in AXES)

    if last >= 0 and SIZE[order[last]] == 4:
        axis = order[last]
        if at[axis] == 1:
            found.append((child(axis, 2), axis, 1, 0))
        if at[axis] == 3:
            found.append((child(axis, 2), axis, -1, 1))
    for i in range(last + 1, 3):
        axis = order[i]
        found.append((child(axis, 1), axis, 1, None))
        if SIZE[axis] == 4:
            found.append((child(axis, 3), axis, -1, None))
    return found


def parents(order):
    found = {}
    for off in OFFSETS:
        for kid, axis, step, half in children(order, off):
            found.setdefault(kid, []).append((off, axis, step, half))
    return found


def span(color, half):
    start, rows = ROWS[color]
    if half is None:
        return start, rows
    return start + half * (rows // 2), rows // 2


def plan(rate=46500.0, delay=1.8):
    free = {("x", 1): 0.0, ("x", -1): 0.0, ("y", 1): 0.0, ("y", -1): 0.0, ("z", 1): 0.0, ("h", 1): 0.0}
    arrive = {}
    piece = 128 * 896

    def move(key, link, now, nbytes):
        free[link] = max(free[link], now) + nbytes / rate
        arrive[key] = free[link] + delay

    def send(kind, color, kid, axis, step, half, now, nbytes):
        move((kind, color, kid, half), (axis, step if SIZE[axis] == 4 else 1), now, nbytes)

    tasks = []
    reduce_up = [parents(order) for order in REDUCE_ORDER]
    gather_up = [parents(order) for order in GATHER_ORDER]
    for color in range(3):
        for off in OFFSETS:
            tasks.append(("ag", color, off))
            tasks.append(("rs", color, off))
    for oy in range(4):
        for color in range(3):
            tasks.append(("gw", color, oy))
    for ox in range(4):
        for oy in range(4):
            tasks.append(("pp", ox, oy))
        for kind in ("g1", "g2", "g3", "gh"):
            tasks.append((kind, ox, 0))
    distance = (0, 1, 2, 1)
    done = {}
    now = 2.5
    arrive[("g1", 0)] = 3.0
    move(("g1", 1), ("x", 1), now, piece)
    move(("g1", 3), ("x", -1), now, piece)
    move(("g1", 2), ("x", 1), now, 2 * piece)
    program = []

    def ready(task):
        kind, first, off = task
        if kind == "ag":
            if off == (0, 0, 0):
                return 2.5
            need = [("ag", first, off, half) for _, _, _, half in gather_up[first][off]]
        elif kind == "rs":
            if ("pp", off[0], off[1]) not in done:
                return None
            need = [("rs", first, kid, half) for kid, _, _, half in children(REDUCE_ORDER[first], off)]
        elif kind == "pp":
            if ("gh", first, 0) not in done or ("g3", first, 0) not in done:
                return None
            need = []
        elif kind == "gw":
            if any(("ag", first, (a, off, c)) not in done for a in range(4) for c in range(2)):
                return None
            if any(("gh", a, 0) not in done for a in range(4)):
                return None
            need = []
        else:
            need = [(kind, first)]
        if any(n not in arrive for n in need):
            return None
        return max([arrive[n] for n in need], default=0.0)

    def rank(task, at):
        kind = task[0]
        if kind[0] == "g" and kind != "gw":
            return (0, at, str(task))
        if kind in ("ag", "rs"):
            return (1, at, str(task))
        if kind == "pp":
            return (2, -(distance[task[1]] + distance[task[2]]), str(task))
        return (3, 0.0, str(task))

    cost = {"ag": 0.05, "rs": 0.4, "pp": 0.9, "gw": 1.2, "g1": 0.05, "g2": 0.05, "g3": 0.05, "gh": 0.05}
    while tasks:
        options = [(ready(t), t) for t in tasks]
        options = [(r, t) for r, t in options if r is not None]
        open_now = [(r, t) for r, t in options if r <= now]
        if not open_now:
            now = min(r for r, _ in options)
            continue
        _, task = min(open_now, key=lambda item: rank(item[1], item[0]))
        tasks.remove(task)
        program.append(task)
        kind, first, off = task
        now += cost[kind]
        done[task] = now
        if kind == "g1":
            move(("g2", first), ("h", 1), now, piece)
        if kind == "g2":
            move(("g3", first), ("z", 1), now, piece)
        if kind == "g3":
            arrive[("gh", first)] = now + 2.0
        if kind == "ag":
            for kid, axis, step, half in children(GATHER_ORDER[first], off):
                send("ag", first, kid, axis, step, half, now, span(first, half)[1] * 256)
        if kind == "rs" and off != (0, 0, 0):
            for _, axis, step, half in reduce_up[first][off]:
                send("rs", first, off, axis, -step, half, now, coded(first, half)[1] * 256)
    return program, now


CHUNK = 64
BLOCK = 1024 + 3 * 16
LAND = 1024 + 3 * 32
TOP = 125.0
LN2 = 0.6931471805599453


def coded(color, half):
    start, rows = ROWS[color]
    base = start + 16 * color
    if half is None:
        return base, rows + 16
    return base + half * (rows // 2), rows // 2 + 16


def body(x_ref, go_ref, w_ref, gi_ref, gw_ref, w_buf, x_all, g_all, part, code, landed, stage,
         w_sem, ag_send, ag_recv, rs_send, rs_recv, x_send, p_send, g_recv, out_sem, *, program):
    gx, gy, y = lax.axis_index("gx"), lax.axis_index("gy"), lax.axis_index("gz")
    zl, x = gx // 4, gx % 4
    zh, core = gy // 2, gy % 2
    primary = core == x // 2
    outer = zh == zl

    def neighbour(axis, step):
        if axis == "x":
            return {"gx": zl * 4 + (x + step + 4) % 4, "gy": gy, "gz": y}
        if axis == "y":
            return {"gx": gx, "gy": gy, "gz": (y + step + 4) % 4}
        return {"gx": (1 - zl) * 4 + x, "gy": gy, "gz": y}

    pair = neighbour("z", 1)
    across = {"gx": (1 - zl) * 4 + x, "gy": (1 - zh) * 2 + core, "gz": y}
    sibling = {"gx": gx, "gy": zh * 2 + 1 - core, "gz": y}

    def pick(a, b):
        if isinstance(a, dict):
            return {k: jnp.where(outer, a[k], b[k]) for k in a}
        return jnp.where(outer, a, b)

    def remote(src, dst, send_sem, recv_sem, device):
        return pltpu.make_async_remote_copy(
            src_ref=src, dst_ref=dst, send_sem=send_sem, recv_sem=recv_sem,
            device_id=device, device_id_type=pl.DeviceIdType.MESH)

    greeted = [neighbour("x", 1), neighbour("x", -1), neighbour("x", 2), neighbour("y", 1), neighbour("y", -1),
               pair, across, sibling]
    barrier = pltpu.get_barrier_semaphore()
    for device in greeted:
        pl.semaphore_signal(barrier, inc=1, device_id=device, device_id_type=pl.DeviceIdType.MESH)

    w_copy = pltpu.make_async_copy(w_ref, w_buf, w_sem)
    w_copy.start()
    x_all[gx * 4 + y] = x_ref[...].T
    pl.semaphore_wait(barrier, len(greeted))

    def first_hop(half, start):
        to_x = 2 * core + half
        src = go_ref.at[:, pl.ds(half * 896, 896)]
        dst = g_all.at[pick(zl * 4 + x, 8 + x)]

        if start:
            @pl.when(to_x == x)
            def _():
                pltpu.make_async_copy(src, dst, g_recv.at[x]).start()

        @pl.when(to_x != x)
        def _():
            copy = remote(src, dst, x_send.at[half], g_recv.at[x], {"gx": zl * 4 + to_x, "gy": gy, "gz": y})
            if start:
                copy.start()
            else:
                copy.wait_send()

    first_hop(0, True)
    first_hop(1, True)

    def landed_g(slot, sem):
        pltpu.make_async_copy(g_all.at[slot], g_all.at[slot], g_recv.at[sem]).wait()

    def passes(kind, ox):
        fx = (x + 4 - ox) % 4
        mine, other = zl * 4 + fx, (1 - zl) * 4 + fx
        if kind == "g1":
            at = pick(mine, 8 + fx)
            return at, fx, [
                remote(g_all.at[at], g_all.at[pick(8 + fx, mine)], p_send.at[ox * 4], g_recv.at[4 + fx], across),
                remote(g_all.at[at], g_all.at[mine], p_send.at[ox * 4 + 1], g_recv.at[pick(12 + mine, 8 + fx)],
                       pick(sibling, pair))]
        if kind == "g2":
            at = pick(8 + fx, other)
            return at, 4 + fx, [
                remote(g_all.at[at], g_all.at[other], p_send.at[ox * 4 + 2], g_recv.at[pick(8 + fx, 12 + other)],
                       pick(pair, sibling))]
        at = pick(other, mine)
        return at, 8 + fx, [
            remote(g_all.at[at], g_all.at[at], p_send.at[ox * 4 + 3], g_recv.at[12 + at], sibling)]

    def spread(kind, ox):
        if kind == "gh":
            @pl.when(jnp.logical_not(primary))
            def _():
                fx = (x + 4 - ox) % 4
                landed_g(fx, 12 + fx)
                landed_g(4 + fx, 16 + fx)
            return

        @pl.when(primary)
        def _():
            at, sem, copies = passes(kind, ox)
            landed_g(at, sem)
            for copy in copies:
                copy.start()

    def gather_slot(off):
        return ((zl + off[2]) % 2 * 4 + (x + 4 - off[0]) % 4) * 4 + (y + 4 - off[1]) % 4

    gather_up = [parents(order) for order in GATHER_ORDER]
    reduce_up = [parents(order) for order in REDUCE_ORDER]

    def sem_id(color, off, half):
        return (color * 32 + index_of(off)) * 2 + (half or 0)

    def gather(color, off):
        slot = gather_slot(off)
        if off != (0, 0, 0):
            for _, axis, step, half in gather_up[color][off]:
                start, rows = span(color, half)
                view = x_all.at[slot, pl.ds(start, rows), :]
                remote(view, view, ag_send, ag_recv.at[sem_id(color, off, half)], neighbour(axis, -step)).wait_recv()
        for kid, axis, step, half in children(GATHER_ORDER[color], off):
            start, rows = span(color, half)
            view = x_all.at[slot, pl.ds(start, rows), :]
            remote(view, view, ag_send, ag_recv.at[sem_id(color, kid, half)], neighbour(axis, step)).start()

    def products(ox, oy):
        to_x, to_y = (x + 4 - ox) % 4, (y + 4 - oy) % 4
        units = jnp.concatenate([g_all[zl * 4 + to_x], g_all[(1 - zl) * 4 + to_x]], axis=0)
        base = index_of((ox, oy, 0))

        def tile(i, carry):
            lines = pl.ds(pl.multiple_of(to_y * 1024 + i * 256, 256), 256)
            got = lax.dot_general(w_buf[lines, :], units, (((1,), (1,)), ((), ())),
                                  preferred_element_type=jnp.float32)
            into = pl.ds(pl.multiple_of(i * 256, 256), 256)
            part[base, into, :] = got[:, :128]
            part[base + 1, into, :] = got[:, 128:]
            return carry

        lax.fori_loop(0, 4, tile, 0)

    def code_view(off, color, half):
        start, rows = coded(color, half)
        return code.at[pl.ds(index_of(off) * BLOCK + start, rows), :]

    def land_view(off, color, half):
        start, rows = coded(color, half)
        return landed.at[pl.ds(index_of(off) * LAND + start + 16 * color + 16 * (half or 0), rows), :]

    def add_child(color, at, kid, half):
        start, rows = ROWS[color]
        from_row = index_of(kid) * LAND + start + 32 * color + 16 * (half or 0)
        unit = landed[pl.ds(from_row + rows // 2, 16), :][0:1].astype(jnp.float32) * (1.0 / (2 * TOP * LN2))
        for side in (0, 1) if half is None else (half,):
            def chunk(i, carry):
                src = pl.ds(pl.multiple_of(from_row + side * (rows // 2 + 16) + i * CHUNK, 16), CHUNK)
                dst = pl.ds(pl.multiple_of(start + side * (rows // 2) + i * CHUNK, CHUNK), CHUNK)
                got = landed[src, :].astype(jnp.float32)
                size = (jnp.log(jnp.abs(got)) + TOP * LN2) * unit
                part[at, dst, :] = part[at, dst, :] + jnp.where(got < 0, -size, size)
                return carry

            lax.fori_loop(0, rows // 2 // CHUNK, chunk, 0)

    def encode(color, at):
        start, rows = ROWS[color]

        def largest(i, carry):
            view = part[at, pl.ds(pl.multiple_of(start + i * CHUNK, CHUNK), CHUNK), :]
            return jnp.maximum(carry, jnp.max(jnp.abs(view).reshape(CHUNK // 8, 8, 128), axis=0))

        most = lax.fori_loop(0, rows // CHUNK, largest, jnp.zeros((8, 128), jnp.float32))
        most = jnp.max(most, axis=0, keepdims=True)
        scale = jnp.maximum(most * 1.01, 1e-35).astype(jnp.bfloat16)
        unit = (2 * TOP) / scale.astype(jnp.float32)
        to_row = at * BLOCK + start + 16 * color
        code[pl.ds(to_row + rows // 2, 16), :] = jnp.broadcast_to(scale, (16, 128))
        for side in range(2):
            def chunk(i, carry):
                src = pl.ds(pl.multiple_of(start + side * (rows // 2) + i * CHUNK, CHUNK), CHUNK)
                dst = pl.ds(pl.multiple_of(to_row + side * (rows // 2 + 16) + i * CHUNK, 16), CHUNK)
                value = part[at, src, :]
                size = lax.exp2(jnp.abs(value) * unit - TOP)
                code[dst, :] = jnp.where(value < 0, -size, size).astype(jnp.bfloat16)
                return carry

            lax.fori_loop(0, rows // 2 // CHUNK, chunk, 0)

    def reduce(color, off):
        at = index_of(off)
        for kid, axis, step, half in children(REDUCE_ORDER[color], off):
            src = land_view(kid, color, half)
            remote(src, src, rs_send, rs_recv.at[sem_id(color, kid, half)], neighbour(axis, step)).wait_recv()
            add_child(color, at, kid, half)
        if off != (0, 0, 0):
            encode(color, at)
            for _, axis, step, half in reduce_up[color][off]:
                remote(code_view(off, color, half), land_view(off, color, half), rs_send,
                       rs_recv.at[sem_id(color, off, half)], neighbour(axis, -step)).start()

    staged = []

    def weights(color, oy):
        start, rows = ROWS[color]
        from_y = (y + 4 - oy) % 4
        slot = len(staged) % 2
        if len(staged) >= 2:
            staged[-2].wait()
        left = jnp.concatenate([x_all[i * 4 + from_y, pl.ds(start, rows), :] for i in range(8)], axis=1)
        got = jnp.dot(left, g_all[pl.ds(0, 8)].reshape(1024, 896), preferred_element_type=jnp.float32)
        stage[slot, pl.ds(0, rows), :] = got.astype(jnp.bfloat16)
        copy = pltpu.make_async_copy(
            stage.at[slot, pl.ds(0, rows), :],
            gw_ref.at[pl.ds(pl.multiple_of(from_y * 1024 + start, 128), rows), :], out_sem.at[slot])
        copy.start()
        staged.append(copy)

    has_w = False
    for kind, first, off in program:
        if kind == "ag":
            gather(first, off)
        elif kind == "rs":
            reduce(first, off)
        elif kind == "gw":
            weights(first, off)
        elif kind == "pp":
            if not has_w:
                w_copy.wait()
                has_w = True
            products(first, off)
        else:
            spread(kind, first)

    gi_ref[...] = part[0].T.astype(jnp.bfloat16)

    for copy in staged[-2:]:
        copy.wait()
    first_hop(0, False)
    first_hop(1, False)

    @pl.when(primary)
    def _():
        for kind in ("g1", "g2", "g3"):
            for ox in range(4):
                for copy in passes(kind, ox)[2]:
                    copy.wait_send()

    sent = x_all.at[pl.ds(0, 31)]
    pltpu.make_async_copy(sent, sent, ag_send).wait()
    rows = sum(coded(color, half)[1] for color in range(3) for ups in reduce_up[color].values() for _, _, _, half in ups)
    sent = code.at[pl.ds(0, rows), :]
    pltpu.make_async_copy(sent, sent, rs_send).wait()


def local(x_saved, grad_out, weight):
    program, _ = plan()
    vmem = pl.BlockSpec(memory_space=pltpu.VMEM)
    anywhere = pl.BlockSpec(memory_space=pl.ANY)
    return pl.pallas_call(
        functools.partial(body, program=program),
        out_shape=(pltpu.VMEM((128, 1024), jnp.bfloat16),
                   jax.ShapeDtypeStruct((4096, 896), jnp.bfloat16)),
        in_specs=[vmem, vmem, anywhere],
        out_specs=(vmem, anywhere),
        scratch_shapes=[
            pltpu.VMEM((4096, 896), jnp.bfloat16),
            pltpu.VMEM((32, 1024, 128), jnp.bfloat16),
            pltpu.VMEM((12, 128, 896), jnp.bfloat16),
            pltpu.VMEM((32, 1024, 128), jnp.float32),
            pltpu.VMEM((32 * BLOCK, 128), jnp.bfloat16),
            pltpu.VMEM((32 * LAND, 128), jnp.bfloat16),
            pltpu.VMEM((2, 384, 896), jnp.bfloat16),
            pltpu.SemaphoreType.DMA,
            pltpu.SemaphoreType.DMA,
            pltpu.SemaphoreType.DMA((192,)),
            pltpu.SemaphoreType.DMA,
            pltpu.SemaphoreType.DMA((192,)),
            pltpu.SemaphoreType.DMA((2,)),
            pltpu.SemaphoreType.DMA((16,)),
            pltpu.SemaphoreType.DMA((20,)),
            pltpu.SemaphoreType.DMA((2,)),
        ],
        compiler_params=pltpu.CompilerParams(collective_id=0, has_side_effects=True, vmem_limit_bytes=63 * 1024 * 1024),
    )(x_saved, grad_out, weight)


def solution(mesh):
    return jax.shard_map(
        local,
        mesh=mesh,
        in_specs=(P("gx", ("gy", "gz")), P("gx", ("gz", "gy")), P("gy", ("gz", "gx"))),
        out_specs=(P("gx", ("gy", "gz")), P("gy", ("gz", "gx"))),
        check_vma=False,
    )
```

```python
import functools

import jax
import jax.numpy as jnp
from jax import lax
from jax.experimental import pallas as pl
from jax.experimental.pallas import tpu as pltpu
from jax.sharding import PartitionSpec as P

SIZE = {"x": 4, "y": 4, "z": 2}
AXES = ("x", "y", "z")
ROWS = ((0, 256), (256, 384), (640, 384))
GATHER_ORDER = (("x", "y", "z"), ("y", "z", "x"), ("z", "x", "y"))
REDUCE_ORDER = (("y", "x", "z"), ("x", "z", "y"), ("z", "y", "x"))
OFFSETS = tuple((a, b, c) for a in range(4) for b in range(4) for c in range(2))


def index_of(off):
    return (off[0] * 4 + off[1]) * 2 + off[2]


def children(order, off):
    at = dict(zip(AXES, off))
    last = max([i for i in range(3) if at[order[i]]], default=-1)
    found = []

    def child(axis, value):
        moved = dict(at)
        moved[axis] = value
        return tuple(moved[a] for a in AXES)

    if last >= 0 and SIZE[order[last]] == 4:
        axis = order[last]
        if at[axis] == 1:
            found.append((child(axis, 2), axis, 1, 0))
        if at[axis] == 3:
            found.append((child(axis, 2), axis, -1, 1))
    for i in range(last + 1, 3):
        axis = order[i]
        found.append((child(axis, 1), axis, 1, None))
        if SIZE[axis] == 4:
            found.append((child(axis, 3), axis, -1, None))
    return found


def parents(order):
    found = {}
    for off in OFFSETS:
        for kid, axis, step, half in children(order, off):
            found.setdefault(kid, []).append((off, axis, step, half))
    return found


def span(color, half):
    start, rows = ROWS[color]
    if half is None:
        return start, rows
    return start + half * (rows // 2), rows // 2


ORDER = (
    0, 128, 208, 64, 216, 209, 130, 48, 4, 210, 68, 176, 2, 224, 232, 144, 76, 178, 116, 211, 134, 225, 146, 70,
    233, 124, 205, 66, 217, 16, 204, 12, 7, 50, 84, 226, 72, 156, 234, 160, 227, 162, 223, 222, 142, 78, 182,
    235, 107, 43, 175, 218, 8, 206, 28, 219, 215, 105, 132, 126, 213, 173, 171, 174, 20, 75, 74, 32, 221, 112,
    118, 18, 165, 140, 86, 39, 109, 220, 101, 229, 169, 167, 150, 92, 35, 214, 60, 111, 73, 230, 207, 181, 6,
    82, 155, 14, 31, 34, 172, 11, 27, 121, 91, 52, 159, 187, 190, 77, 228, 123, 188, 47, 37, 15, 180, 114, 87,
    80, 100, 161, 185, 164, 41, 30, 231, 36, 163, 103, 59, 122, 212, 44, 153, 189, 22, 69, 191, 149, 23, 119,
    117, 38, 120, 127, 19, 54, 138, 151, 89, 158, 98, 145, 203, 51, 96, 148, 57, 95, 99, 194, 71, 46, 136, 139,
    137, 62, 168, 40, 183, 21, 115, 166, 45, 94, 193, 201, 25, 63, 79, 83, 55, 90, 10, 179, 152, 108, 88, 197,
    157, 143, 85, 56, 110, 97, 102, 135, 93, 3, 147, 125, 106, 186, 61, 133, 202, 9, 184, 33, 29, 24, 141, 42,
    53, 154, 67, 177, 196, 81, 131, 192, 104, 58, 113, 170, 5, 17, 26, 13, 49, 195, 198, 199, 200, 129, 65, 1
)


def plan():
    tasks = []
    for color in range(3):
        for off in OFFSETS:
            tasks.append(("ag", color, off))
            tasks.append(("rs", color, off))
    for oy in range(4):
        for color in range(3):
            tasks.append(("gw", color, oy))
    for ox in range(4):
        for oy in range(4):
            tasks.append(("pp", ox, oy))
        for kind in ("g1", "g2", "g3", "gh"):
            tasks.append((kind, ox, 0))
    return [tasks[i] for i in ORDER]


CHUNK = 64
BLOCK = 1024 + 3 * 16
LAND = 1024 + 3 * 32
TOP = 125.0
LN2 = 0.6931471805599453


def coded(color, half):
    start, rows = ROWS[color]
    base = start + 16 * color
    if half is None:
        return base, rows + 16
    return base + half * (rows // 2), rows // 2 + 16


def body(x_ref, go_ref, w_ref, gi_ref, gw_ref, w_buf, x_all, g_all, part, code, landed,
         w_sem, ag_send, ag_recv, rs_send, rs_recv, x_send, p_send, g_recv, *, program):
    gx, gy, y = lax.axis_index("gx"), lax.axis_index("gy"), lax.axis_index("gz")
    zl, x = gx // 4, gx % 4
    zh, core = gy // 2, gy % 2
    primary = core == x // 2
    outer = zh == zl

    def neighbour(axis, step):
        if axis == "x":
            return {"gx": zl * 4 + (x + step + 4) % 4, "gy": gy, "gz": y}
        if axis == "y":
            return {"gx": gx, "gy": gy, "gz": (y + step + 4) % 4}
        return {"gx": (1 - zl) * 4 + x, "gy": gy, "gz": y}

    pair = neighbour("z", 1)
    across = {"gx": (1 - zl) * 4 + x, "gy": (1 - zh) * 2 + core, "gz": y}
    sibling = {"gx": gx, "gy": zh * 2 + 1 - core, "gz": y}

    def pick(a, b):
        if isinstance(a, dict):
            return {k: jnp.where(outer, a[k], b[k]) for k in a}
        return jnp.where(outer, a, b)

    def remote(src, dst, send_sem, recv_sem, device):
        return pltpu.make_async_remote_copy(
            src_ref=src, dst_ref=dst, send_sem=send_sem, recv_sem=recv_sem,
            device_id=device, device_id_type=pl.DeviceIdType.MESH)

    greeted = [neighbour("x", 1), neighbour("x", -1), neighbour("x", 2), neighbour("y", 1), neighbour("y", -1),
               pair, across, sibling]
    barrier = pltpu.get_barrier_semaphore()
    for device in greeted:
        pl.semaphore_signal(barrier, inc=1, device_id=device, device_id_type=pl.DeviceIdType.MESH)

    w_copy = pltpu.make_async_copy(w_ref, w_buf, w_sem)
    w_copy.start()
    x_all[gx * 4 + y] = x_ref[...].T
    pl.semaphore_wait(barrier, len(greeted))

    def first_hop(half, start):
        to_x = 2 * core + half
        src = go_ref.at[:, pl.ds(half * 896, 896)]
        dst = g_all.at[pick(zl * 4 + x, 8 + x)]

        if start:
            @pl.when(to_x == x)
            def _():
                pltpu.make_async_copy(src, dst, g_recv.at[x]).start()

        @pl.when(to_x != x)
        def _():
            copy = remote(src, dst, x_send.at[half], g_recv.at[x], {"gx": zl * 4 + to_x, "gy": gy, "gz": y})
            if start:
                copy.start()
            else:
                copy.wait_send()

    first_hop(0, True)
    first_hop(1, True)

    def landed_g(slot, sem):
        pltpu.make_async_copy(g_all.at[slot], g_all.at[slot], g_recv.at[sem]).wait()

    def passes(kind, ox):
        fx = (x + 4 - ox) % 4
        mine, other = zl * 4 + fx, (1 - zl) * 4 + fx
        if kind == "g1":
            at = pick(mine, 8 + fx)
            return at, fx, [
                remote(g_all.at[at], g_all.at[pick(8 + fx, mine)], p_send.at[ox * 4], g_recv.at[4 + fx], across),
                remote(g_all.at[at], g_all.at[mine], p_send.at[ox * 4 + 1], g_recv.at[pick(12 + mine, 8 + fx)],
                       pick(sibling, pair))]
        if kind == "g2":
            at = pick(8 + fx, other)
            return at, 4 + fx, [
                remote(g_all.at[at], g_all.at[other], p_send.at[ox * 4 + 2], g_recv.at[pick(8 + fx, 12 + other)],
                       pick(pair, sibling))]
        at = pick(other, mine)
        return at, 8 + fx, [
            remote(g_all.at[at], g_all.at[at], p_send.at[ox * 4 + 3], g_recv.at[12 + at], sibling)]

    def spread(kind, ox):
        if kind == "gh":
            @pl.when(jnp.logical_not(primary))
            def _():
                fx = (x + 4 - ox) % 4
                landed_g(fx, 12 + fx)
                landed_g(4 + fx, 16 + fx)
            return

        @pl.when(primary)
        def _():
            at, sem, copies = passes(kind, ox)
            landed_g(at, sem)
            for copy in copies:
                copy.start()

    def gather_slot(off):
        return ((zl + off[2]) % 2 * 4 + (x + 4 - off[0]) % 4) * 4 + (y + 4 - off[1]) % 4

    gather_up = [parents(order) for order in GATHER_ORDER]
    reduce_up = [parents(order) for order in REDUCE_ORDER]

    def sem_id(color, off, half):
        return (color * 32 + index_of(off)) * 2 + (half or 0)

    def gather(color, off):
        slot = gather_slot(off)
        if off != (0, 0, 0):
            for _, axis, step, half in gather_up[color][off]:
                start, rows = span(color, half)
                view = x_all.at[slot, pl.ds(start, rows), :]
                remote(view, view, ag_send, ag_recv.at[sem_id(color, off, half)], neighbour(axis, -step)).wait_recv()
        for kid, axis, step, half in children(GATHER_ORDER[color], off):
            start, rows = span(color, half)
            view = x_all.at[slot, pl.ds(start, rows), :]
            remote(view, view, ag_send, ag_recv.at[sem_id(color, kid, half)], neighbour(axis, step)).start()

    def products(ox, oy):
        to_x, to_y = (x + 4 - ox) % 4, (y + 4 - oy) % 4
        units = jnp.concatenate([g_all[zl * 4 + to_x], g_all[(1 - zl) * 4 + to_x]], axis=0)
        base = index_of((ox, oy, 0))

        def tile(i, carry):
            lines = pl.ds(pl.multiple_of(to_y * 1024 + i * 256, 256), 256)
            got = lax.dot_general(w_buf[lines, :], units, (((1,), (1,)), ((), ())),
                                  preferred_element_type=jnp.float32)
            into = pl.ds(pl.multiple_of(i * 256, 256), 256)
            part[base, into, :] = got[:, :128]
            part[base + 1, into, :] = got[:, 128:]
            return carry

        lax.fori_loop(0, 4, tile, 0)

    def code_view(off, color, half):
        start, rows = coded(color, half)
        return code.at[pl.ds(index_of(off) * BLOCK + start, rows), :]

    def land_view(off, color, half):
        start, rows = coded(color, half)
        return landed.at[pl.ds(index_of(off) * LAND + start + 16 * color + 16 * (half or 0), rows), :]

    def add_child(color, at, kid, half):
        start, rows = ROWS[color]
        from_row = index_of(kid) * LAND + start + 32 * color + 16 * (half or 0)
        unit = landed[pl.ds(from_row + rows // 2, 16), :][0:1].astype(jnp.float32) * (1.0 / (2 * TOP * LN2))
        for side in (0, 1) if half is None else (half,):
            def chunk(i, carry):
                src = pl.ds(pl.multiple_of(from_row + side * (rows // 2 + 16) + i * CHUNK, 16), CHUNK)
                dst = pl.ds(pl.multiple_of(start + side * (rows // 2) + i * CHUNK, CHUNK), CHUNK)
                got = landed[src, :].astype(jnp.float32)
                size = (jnp.log(jnp.abs(got)) + TOP * LN2) * unit
                part[at, dst, :] = part[at, dst, :] + jnp.where(got < 0, -size, size)
                return carry

            lax.fori_loop(0, rows // 2 // CHUNK, chunk, 0)

    def encode(color, at):
        start, rows = ROWS[color]

        def largest(i, carry):
            view = part[at, pl.ds(pl.multiple_of(start + i * CHUNK, CHUNK), CHUNK), :]
            return jnp.maximum(carry, jnp.max(jnp.abs(view).reshape(CHUNK // 8, 8, 128), axis=0))

        most = lax.fori_loop(0, rows // CHUNK, largest, jnp.zeros((8, 128), jnp.float32))
        most = jnp.max(most, axis=0, keepdims=True)
        scale = jnp.maximum(most * 1.01, 1e-35).astype(jnp.bfloat16)
        unit = (2 * TOP) / scale.astype(jnp.float32)
        to_row = at * BLOCK + start + 16 * color
        code[pl.ds(to_row + rows // 2, 16), :] = jnp.broadcast_to(scale, (16, 128))
        for side in range(2):
            def chunk(i, carry):
                src = pl.ds(pl.multiple_of(start + side * (rows // 2) + i * CHUNK, CHUNK), CHUNK)
                dst = pl.ds(pl.multiple_of(to_row + side * (rows // 2 + 16) + i * CHUNK, 16), CHUNK)
                value = part[at, src, :]
                size = lax.exp2(jnp.abs(value) * unit - TOP)
                code[dst, :] = jnp.where(value < 0, -size, size).astype(jnp.bfloat16)
                return carry

            lax.fori_loop(0, rows // 2 // CHUNK, chunk, 0)

    def reduce(color, off):
        at = index_of(off)
        for kid, axis, step, half in children(REDUCE_ORDER[color], off):
            src = land_view(kid, color, half)
            remote(src, src, rs_send, rs_recv.at[sem_id(color, kid, half)], neighbour(axis, step)).wait_recv()
            add_child(color, at, kid, half)
        if off != (0, 0, 0):
            encode(color, at)
            for _, axis, step, half in reduce_up[color][off]:
                remote(code_view(off, color, half), land_view(off, color, half), rs_send,
                       rs_recv.at[sem_id(color, off, half)], neighbour(axis, -step)).start()

    def weights(color, oy):
        start, rows = ROWS[color]
        from_y = (y + 4 - oy) % 4
        left = jnp.concatenate([x_all[i * 4 + from_y, pl.ds(start, rows), :] for i in range(8)], axis=1)
        got = jnp.dot(left, g_all[pl.ds(0, 8)].reshape(1024, 896), preferred_element_type=jnp.float32)
        gw_ref[pl.ds(pl.multiple_of(from_y * 1024 + start, 128), rows), :] = got.astype(jnp.bfloat16)

    has_w = False
    for kind, first, off in program:
        if kind == "ag":
            gather(first, off)
        elif kind == "rs":
            reduce(first, off)
        elif kind == "gw":
            weights(first, off)
        elif kind == "pp":
            if not has_w:
                w_copy.wait()
                has_w = True
            products(first, off)
        else:
            spread(kind, first)

    gi_ref[...] = part[0].T.astype(jnp.bfloat16)

    first_hop(0, False)
    first_hop(1, False)

    @pl.when(primary)
    def _():
        for kind in ("g1", "g2", "g3"):
            for ox in range(4):
                for copy in passes(kind, ox)[2]:
                    copy.wait_send()

    sent = x_all.at[pl.ds(0, 31)]
    pltpu.make_async_copy(sent, sent, ag_send).wait()
    rows = sum(coded(color, half)[1] for color in range(3) for ups in reduce_up[color].values() for _, _, _, half in ups)
    sent = code.at[pl.ds(0, rows), :]
    pltpu.make_async_copy(sent, sent, rs_send).wait()


def local(x_saved, grad_out, weight):
    program = plan()
    vmem = pl.BlockSpec(memory_space=pltpu.VMEM)
    anywhere = pl.BlockSpec(memory_space=pl.ANY)
    return pl.pallas_call(
        functools.partial(body, program=program),
        out_shape=(pltpu.VMEM((128, 1024), jnp.bfloat16),
                   pltpu.VMEM((4096, 896), jnp.bfloat16)),
        in_specs=[vmem, vmem, anywhere],
        out_specs=(vmem, vmem),
        scratch_shapes=[
            pltpu.VMEM((4096, 896), jnp.bfloat16),
            pltpu.VMEM((32, 1024, 128), jnp.bfloat16),
            pltpu.VMEM((12, 128, 896), jnp.bfloat16),
            pltpu.VMEM((32, 1024, 128), jnp.float32),
            pltpu.VMEM((32 * BLOCK, 128), jnp.bfloat16),
            pltpu.VMEM((32 * LAND, 128), jnp.bfloat16),
            pltpu.SemaphoreType.DMA,
            pltpu.SemaphoreType.DMA,
            pltpu.SemaphoreType.DMA((192,)),
            pltpu.SemaphoreType.DMA,
            pltpu.SemaphoreType.DMA((192,)),
            pltpu.SemaphoreType.DMA((2,)),
            pltpu.SemaphoreType.DMA((16,)),
            pltpu.SemaphoreType.DMA((20,)),
        ],
        compiler_params=pltpu.CompilerParams(collective_id=0, has_side_effects=True, vmem_limit_bytes=53 * 1024 * 1024),
    )(x_saved, grad_out, weight)


def solution(mesh):
    return jax.shard_map(
        local,
        mesh=mesh,
        in_specs=(P("gx", ("gy", "gz")), P("gx", ("gz", "gy")), P("gy", ("gz", "gx"))),
        out_specs=(P("gx", ("gy", "gz")), P("gy", ("gz", "gx"))),
        check_vma=False,
    )
```

```python
import functools

import jax
import jax.numpy as jnp
from jax import lax
from jax.experimental import pallas as pl
from jax.experimental.pallas import tpu as pltpu
from jax.sharding import PartitionSpec as P

SIZE = {"x": 4, "y": 4, "z": 2}
AXES = ("x", "y", "z")
ROWS = ((0, 256), (256, 384), (640, 384))
GATHER_ORDER = (("x", "y", "z"), ("y", "z", "x"), ("z", "x", "y"))
REDUCE_ORDER = GATHER_ORDER
OFFSETS = tuple((a, b, c) for a in range(4) for b in range(4) for c in range(2))


def index_of(off):
    return (off[0] * 4 + off[1]) * 2 + off[2]


def children(order, off):
    at = dict(zip(AXES, off))
    last = max([i for i in range(3) if at[order[i]]], default=-1)
    found = []

    def child(axis, value):
        moved = dict(at)
        moved[axis] = value
        return tuple(moved[a] for a in AXES)

    if last >= 0 and SIZE[order[last]] == 4:
        axis = order[last]
        if at[axis] == 1:
            found.append((child(axis, 2), axis, 1, 0))
        if at[axis] == 3:
            found.append((child(axis, 2), axis, -1, 1))
    for i in range(last + 1, 3):
        axis = order[i]
        found.append((child(axis, 1), axis, 1, None))
        if SIZE[axis] == 4:
            found.append((child(axis, 3), axis, -1, None))
    return found


def parents(order):
    found = {}
    for off in OFFSETS:
        for kid, axis, step, half in children(order, off):
            found.setdefault(kid, []).append((off, axis, step, half))
    return found


def span(color, half):
    start, rows = ROWS[color]
    if half is None:
        return start, rows
    return start + half * (rows // 2), rows // 2


ORDER = (
    0, 128, 208, 64, 209, 216, 130, 232, 48, 176, 68, 76, 224, 16, 210, 60, 144, 211, 178, 225, 70, 205, 206,
    217, 146, 72, 137, 28, 116, 180, 132, 207, 233, 226, 156, 190, 158, 66, 80, 218, 227, 20, 182, 52, 139, 222,
    74, 107, 32, 204, 84, 124, 171, 219, 140, 214, 43, 24, 223, 142, 30, 12, 169, 134, 221, 56, 143, 78, 188,
    234, 103, 27, 213, 120, 101, 162, 34, 235, 86, 220, 44, 91, 111, 148, 136, 100, 99, 2, 126, 4, 135, 118, 23,
    109, 230, 175, 82, 41, 153, 152, 36, 47, 160, 59, 212, 114, 8, 123, 94, 112, 167, 54, 88, 150, 92, 187, 229,
    165, 87, 22, 25, 14, 83, 228, 138, 215, 105, 35, 155, 18, 40, 173, 174, 39, 185, 122, 90, 231, 46, 7, 6,
    191, 63, 57, 119, 11, 194, 166, 62, 172, 50, 104, 75, 164, 15, 127, 121, 95, 151, 31, 115, 159, 125, 184,
    10, 89, 189, 97, 38, 203, 42, 157, 183, 163, 61, 26, 21, 192, 45, 98, 110, 181, 96, 161, 85, 193, 37, 102,
    168, 58, 55, 79, 9, 93, 106, 51, 108, 117, 198, 73, 149, 71, 154, 147, 29, 141, 196, 179, 202, 81, 177, 53,
    5, 195, 19, 33, 67, 199, 170, 186, 133, 77, 145, 131, 113, 13, 69, 197, 3, 17, 49, 200, 201, 65, 129, 1
)


def plan():
    tasks = []
    for color in range(3):
        for off in OFFSETS:
            tasks.append(("ag", color, off))
            tasks.append(("rs", color, off))
    for oy in range(4):
        for color in range(3):
            tasks.append(("gw", color, oy))
    for ox in range(4):
        for oy in range(4):
            tasks.append(("pp", ox, oy))
        for kind in ("g1", "g2", "g3", "gh"):
            tasks.append((kind, ox, 0))
    return [tasks[i] for i in ORDER]


CHUNK = 64
BLOCK = 1024 + 3 * 16
LAND = 1024 + 3 * 32
TOP = 125.0
LN2 = 0.6931471805599453


def coded(color, half):
    start, rows = ROWS[color]
    base = start + 16 * color
    if half is None:
        return base, rows + 16
    return base + half * (rows // 2), rows // 2 + 16


def body(x_ref, go_ref, w_ref, gi_ref, gw_ref, w_buf, x_all, g_all, part, code, landed,
         w_sem, ag_send, ag_recv, rs_send, rs_recv, x_send, p_send, g_recv, *, program):
    gx, gy, y = lax.axis_index("gx"), lax.axis_index("gy"), lax.axis_index("gz")
    zl, x = gx // 4, gx % 4
    zh, core = gy // 2, gy % 2
    primary = core == x // 2
    outer = zh == zl

    def neighbour(axis, step):
        if axis == "x":
            return {"gx": zl * 4 + (x + step + 4) % 4, "gy": gy, "gz": y}
        if axis == "y":
            return {"gx": gx, "gy": gy, "gz": (y + step + 4) % 4}
        return {"gx": (1 - zl) * 4 + x, "gy": gy, "gz": y}

    pair = neighbour("z", 1)
    across = {"gx": (1 - zl) * 4 + x, "gy": (1 - zh) * 2 + core, "gz": y}
    sibling = {"gx": gx, "gy": zh * 2 + 1 - core, "gz": y}

    def pick(a, b):
        if isinstance(a, dict):
            return {k: jnp.where(outer, a[k], b[k]) for k in a}
        return jnp.where(outer, a, b)

    def remote(src, dst, send_sem, recv_sem, device):
        return pltpu.make_async_remote_copy(
            src_ref=src, dst_ref=dst, send_sem=send_sem, recv_sem=recv_sem,
            device_id=device, device_id_type=pl.DeviceIdType.MESH)

    greeted = [neighbour("x", 1), neighbour("x", -1), neighbour("x", 2), neighbour("y", 1), neighbour("y", -1),
               pair, across, sibling]
    barrier = pltpu.get_barrier_semaphore()
    for device in greeted:
        pl.semaphore_signal(barrier, inc=1, device_id=device, device_id_type=pl.DeviceIdType.MESH)

    w_copy = pltpu.make_async_copy(w_ref, w_buf, w_sem)
    w_copy.start()
    x_all[gx * 4 + y] = x_ref[...].T
    pl.semaphore_wait(barrier, len(greeted))

    def first_hop(half, start):
        to_x = 2 * core + half
        src = go_ref.at[:, pl.ds(half * 896, 896)]
        dst = g_all.at[pick(zl * 4 + x, 8 + x)]

        if start:
            @pl.when(to_x == x)
            def _():
                pltpu.make_async_copy(src, dst, g_recv.at[x]).start()

        @pl.when(to_x != x)
        def _():
            copy = remote(src, dst, x_send.at[half], g_recv.at[x], {"gx": zl * 4 + to_x, "gy": gy, "gz": y})
            if start:
                copy.start()
            else:
                copy.wait_send()

    first_hop(0, True)
    first_hop(1, True)

    def landed_g(slot, sem):
        pltpu.make_async_copy(g_all.at[slot], g_all.at[slot], g_recv.at[sem]).wait()

    def passes(kind, ox):
        fx = (x + 4 - ox) % 4
        mine, other = zl * 4 + fx, (1 - zl) * 4 + fx
        if kind == "g1":
            at = pick(mine, 8 + fx)
            return at, fx, [
                remote(g_all.at[at], g_all.at[pick(8 + fx, mine)], p_send.at[ox * 4], g_recv.at[4 + fx], across),
                remote(g_all.at[at], g_all.at[mine], p_send.at[ox * 4 + 1], g_recv.at[pick(12 + mine, 8 + fx)],
                       pick(sibling, pair))]
        if kind == "g2":
            at = pick(8 + fx, other)
            return at, 4 + fx, [
                remote(g_all.at[at], g_all.at[other], p_send.at[ox * 4 + 2], g_recv.at[pick(8 + fx, 12 + other)],
                       pick(pair, sibling))]
        at = pick(other, mine)
        return at, 8 + fx, [
            remote(g_all.at[at], g_all.at[at], p_send.at[ox * 4 + 3], g_recv.at[12 + at], sibling)]

    def spread(kind, ox):
        if kind == "gh":
            @pl.when(jnp.logical_not(primary))
            def _():
                fx = (x + 4 - ox) % 4
                landed_g(fx, 12 + fx)
                landed_g(4 + fx, 16 + fx)
            return

        @pl.when(primary)
        def _():
            at, sem, copies = passes(kind, ox)
            landed_g(at, sem)
            for copy in copies:
                copy.start()

    def gather_slot(off):
        return ((zl + off[2]) % 2 * 4 + (x + 4 - off[0]) % 4) * 4 + (y + 4 - off[1]) % 4

    gather_up = [parents(order) for order in GATHER_ORDER]
    reduce_up = [parents(order) for order in REDUCE_ORDER]

    def sem_id(color, off, half):
        return (color * 32 + index_of(off)) * 2 + (half or 0)

    def gather(color, off):
        slot = gather_slot(off)
        if off != (0, 0, 0):
            for _, axis, step, half in gather_up[color][off]:
                start, rows = span(color, half)
                view = x_all.at[slot, pl.ds(start, rows), :]
                remote(view, view, ag_send, ag_recv.at[sem_id(color, off, half)], neighbour(axis, -step)).wait_recv()
        for kid, axis, step, half in children(GATHER_ORDER[color], off):
            start, rows = span(color, half)
            view = x_all.at[slot, pl.ds(start, rows), :]
            remote(view, view, ag_send, ag_recv.at[sem_id(color, kid, half)], neighbour(axis, step)).start()

    def products(ox, oy):
        to_x, to_y = (x + 4 - ox) % 4, (y + 4 - oy) % 4
        units = jnp.concatenate([g_all[zl * 4 + to_x], g_all[(1 - zl) * 4 + to_x]], axis=0)
        base = index_of((ox, oy, 0))

        def tile(i, carry):
            lines = pl.ds(pl.multiple_of(to_y * 1024 + i * 256, 256), 256)
            got = lax.dot_general(w_buf[lines, :], units, (((1,), (1,)), ((), ())),
                                  preferred_element_type=jnp.float32)
            into = pl.ds(pl.multiple_of(i * 256, 256), 256)
            part[base, into, :] = got[:, :128]
            part[base + 1, into, :] = got[:, 128:]
            return carry

        lax.fori_loop(0, 4, tile, 0)

    def code_view(off, color, half):
        start, rows = coded(color, half)
        return code.at[pl.ds(index_of(off) * BLOCK + start, rows), :]

    def land_view(off, color, half):
        start, rows = coded(color, half)
        return landed.at[pl.ds(index_of(off) * LAND + start + 16 * color + 16 * (half or 0), rows), :]

    def add_child(color, at, kid, half):
        start, rows = ROWS[color]
        from_row = index_of(kid) * LAND + start + 32 * color + 16 * (half or 0)
        unit = landed[pl.ds(from_row + rows // 2, 16), :][0:1].astype(jnp.float32) * (1.0 / (2 * TOP * LN2))
        for side in (0, 1) if half is None else (half,):
            def chunk(i, carry):
                src = pl.ds(pl.multiple_of(from_row + side * (rows // 2 + 16) + i * CHUNK, 16), CHUNK)
                dst = pl.ds(pl.multiple_of(start + side * (rows // 2) + i * CHUNK, CHUNK), CHUNK)
                got = landed[src, :].astype(jnp.float32)
                size = (jnp.log(jnp.abs(got)) + TOP * LN2) * unit
                part[at, dst, :] = part[at, dst, :] + jnp.where(got < 0, -size, size)
                return carry

            lax.fori_loop(0, rows // 2 // CHUNK, chunk, 0)

    def encode(color, at):
        start, rows = ROWS[color]

        def largest(i, carry):
            view = part[at, pl.ds(pl.multiple_of(start + i * CHUNK, CHUNK), CHUNK), :]
            return jnp.maximum(carry, jnp.max(jnp.abs(view).reshape(CHUNK // 8, 8, 128), axis=0))

        most = lax.fori_loop(0, rows // CHUNK, largest, jnp.zeros((8, 128), jnp.float32))
        most = jnp.max(most, axis=0, keepdims=True)
        scale = jnp.maximum(most * 1.01, 1e-35).astype(jnp.bfloat16)
        unit = (2 * TOP) / scale.astype(jnp.float32)
        to_row = at * BLOCK + start + 16 * color
        code[pl.ds(to_row + rows // 2, 16), :] = jnp.broadcast_to(scale, (16, 128))
        for side in range(2):
            def chunk(i, carry):
                src = pl.ds(pl.multiple_of(start + side * (rows // 2) + i * CHUNK, CHUNK), CHUNK)
                dst = pl.ds(pl.multiple_of(to_row + side * (rows // 2 + 16) + i * CHUNK, 16), CHUNK)
                value = part[at, src, :]
                size = lax.exp2(jnp.abs(value) * unit - TOP)
                code[dst, :] = jnp.where(value < 0, -size, size).astype(jnp.bfloat16)
                return carry

            lax.fori_loop(0, rows // 2 // CHUNK, chunk, 0)

    def reduce(color, off):
        at = index_of(off)
        for kid, axis, step, half in children(REDUCE_ORDER[color], off):
            src = land_view(kid, color, half)
            remote(src, src, rs_send, rs_recv.at[sem_id(color, kid, half)], neighbour(axis, step)).wait_recv()
            add_child(color, at, kid, half)
        if off != (0, 0, 0):
            encode(color, at)
            for _, axis, step, half in reduce_up[color][off]:
                remote(code_view(off, color, half), land_view(off, color, half), rs_send,
                       rs_recv.at[sem_id(color, off, half)], neighbour(axis, -step)).start()

    def weights(color, oy):
        start, rows = ROWS[color]
        from_y = (y + 4 - oy) % 4
        left = jnp.concatenate([x_all[i * 4 + from_y, pl.ds(start, rows), :] for i in range(8)], axis=1)
        got = jnp.dot(left, g_all[pl.ds(0, 8)].reshape(1024, 896), preferred_element_type=jnp.float32)
        gw_ref[pl.ds(pl.multiple_of(from_y * 1024 + start, 128), rows), :] = got.astype(jnp.bfloat16)

    has_w = False
    for kind, first, off in program:
        if kind == "ag":
            gather(first, off)
        elif kind == "rs":
            reduce(first, off)
        elif kind == "gw":
            weights(first, off)
        elif kind == "pp":
            if not has_w:
                w_copy.wait()
                has_w = True
            products(first, off)
        else:
            spread(kind, first)

    gi_ref[...] = part[0].T.astype(jnp.bfloat16)

    first_hop(0, False)
    first_hop(1, False)

    @pl.when(primary)
    def _():
        for kind in ("g1", "g2", "g3"):
            for ox in range(4):
                for copy in passes(kind, ox)[2]:
                    copy.wait_send()

    sent = x_all.at[pl.ds(0, 31)]
    pltpu.make_async_copy(sent, sent, ag_send).wait()
    rows = sum(coded(color, half)[1] for color in range(3) for ups in reduce_up[color].values() for _, _, _, half in ups)
    sent = code.at[pl.ds(0, rows), :]
    pltpu.make_async_copy(sent, sent, rs_send).wait()


def local(x_saved, grad_out, weight):
    program = plan()
    vmem = pl.BlockSpec(memory_space=pltpu.VMEM)
    anywhere = pl.BlockSpec(memory_space=pl.ANY)
    return pl.pallas_call(
        functools.partial(body, program=program),
        out_shape=(pltpu.VMEM((128, 1024), jnp.bfloat16),
                   pltpu.VMEM((4096, 896), jnp.bfloat16)),
        in_specs=[vmem, vmem, anywhere],
        out_specs=(vmem, vmem),
        scratch_shapes=[
            pltpu.VMEM((4096, 896), jnp.bfloat16),
            pltpu.VMEM((32, 1024, 128), jnp.bfloat16),
            pltpu.VMEM((12, 128, 896), jnp.bfloat16),
            pltpu.VMEM((32, 1024, 128), jnp.float32),
            pltpu.VMEM((32 * BLOCK, 128), jnp.bfloat16),
            pltpu.VMEM((32 * LAND, 128), jnp.bfloat16),
            pltpu.SemaphoreType.DMA,
            pltpu.SemaphoreType.DMA,
            pltpu.SemaphoreType.DMA((192,)),
            pltpu.SemaphoreType.DMA,
            pltpu.SemaphoreType.DMA((192,)),
            pltpu.SemaphoreType.DMA((2,)),
            pltpu.SemaphoreType.DMA((16,)),
            pltpu.SemaphoreType.DMA((20,)),
        ],
        compiler_params=pltpu.CompilerParams(collective_id=0, has_side_effects=True, vmem_limit_bytes=53 * 1024 * 1024),
    )(x_saved, grad_out, weight)


def solution(mesh):
    return jax.shard_map(
        local,
        mesh=mesh,
        in_specs=(P("gx", ("gy", "gz")), P("gx", ("gz", "gy")), P("gy", ("gz", "gx"))),
        out_specs=(P("gx", ("gy", "gz")), P("gy", ("gz", "gx"))),
        check_vma=False,
    )
```
